768 devices in a mesh: island: 24 (over y_lo, z), tp: 32 (over y_hi, x, core).
Axes of the slice: x: 4, y: 8 (y_hi: 4, y_lo: 2; y = y_hi * 2 + y_lo), z: 12, core: 2. Of those that a mesh axis runs over, the one named last changes fastest.
Arguments:
- tokens: bfloat16 [24, 256, 4096], P('island', 'tp'), may hold values from -6 to 6
- cotangent: bfloat16 [24, 256, 4096], P('island', 'tp'), may hold values from -1.5 to 1.5
- gate_weight: bfloat16 [4096, 7168], P(None, 'tp'), may hold values from -0.09375 to 0.09375
- up_weight: bfloat16 [4096, 7168], P(None, 'tp'), may hold values from -0.09375 to 0.09375
- down_weight: bfloat16 [7168, 4096], P('tp'), may hold values from -0.0625 to 0.0625
- local_fragment: float32 [24, 786432], P('island', 'tp'), may hold values from -9 to 9
- global_fragment: float32 [786432], P('tp'), may hold values from -6 to 6
- outer_velocity: float32 [786432], P('tp'), may hold values from -3 to 3
Outputs:
- layer_out: bfloat16 [24, 256, 4096], P('island', 'tp')
- input_grad: bfloat16 [24, 256, 4096], P('island', 'tp')
- new_fragment: float32 [786432], P('tp')
- new_velocity: float32 [786432], P('tp')
The draws below stay inside these ranges and needn't reach their ends.
All inputs are finite; a program needn't handle non-finite values.
Results may differ from the reference program's by a relative error of at most 0.015.
Values may be sent and summed in bfloat16 or wider, within the bound.
A program may use at most 64 MiB of HBM per device.

```python
import jax
import jax.numpy as jnp
from jax import lax

D = 4096
FF = 7168
TOKENS = 256
ISLANDS = 24
FRAG = 786432
N_ISLAND = 24
N_TP = 32


def fragment_pair(key):
    base = jax.random.fold_in(key, 7177)
    first, second, third = jax.random.split(base, 3)
    global_values = jnp.clip(jax.random.normal(first, (FRAG,), jnp.float32), -6.0, 6.0)
    common = 0.3 * jnp.clip(jax.random.normal(second, (FRAG,), jnp.float32), -4.0, 4.0)
    own = 0.3 * jnp.clip(jax.random.normal(third, (ISLANDS, FRAG), jnp.float32), -4.0, 4.0)
    local_values = global_values[None, :] - common[None, :] - own
    return (global_values, local_values)


def draw_global_fragment(key, part):
    return fragment_pair(key)[0]


def draw_local_fragment(key, part):
    return fragment_pair(key)[1]


def steps_of(rng, dims, pieces, smallest, largest):
    def one(dim, shards_of):
        draws = jax.random.uniform(jax.random.fold_in(jax.random.fold_in(rng, 6), dim), (shards_of,), jnp.float32, smallest / len(pieces), largest / len(pieces))
        return jnp.repeat(jnp.exp(draws), dims[dim] // shards_of).reshape((-1,) + (1,) * (len(dims) - dim - 1))

    factor_of = one(*pieces[0])
    for cut in pieces[1:]:
        factor_of = factor_of * one(*cut)
    return factor_of


def centred(key, extent, scale, bound, cuts=(), kind=jnp.bfloat16):
    drawn = scale * jax.random.normal(key, extent, jnp.float32)
    if cuts:
        drawn = drawn * steps_of(key, extent, cuts, -0.22, 0.18)
    return jnp.clip(drawn, -bound, bound).astype(kind)


def setup_inputs(seed: int = 0) -> dict:
    key_of = jax.random.split(jax.random.key(seed), 9)
    return {
        "tokens": centred(key_of[0], (ISLANDS, TOKENS, D), 1.0, 6.0, ((0, 24), (1, 32))),
        "cotangent": centred(key_of[1], (ISLANDS, TOKENS, D), 0.25, 1.5, ((0, 24), (1, 32))),
        "gate_weight": centred(key_of[2], (D, FF), D ** -0.5, 0.09375, ((1, 32),)),
        "up_weight": centred(key_of[3], (D, FF), D ** -0.5, 0.09375, ((1, 32),)),
        "down_weight": centred(key_of[4], (FF, D), FF ** -0.5, 0.0625, ((0, 32),)),
        "local_fragment": draw_local_fragment(jax.random.fold_in(key_of[8], 71), 0),
        "global_fragment": draw_global_fragment(jax.random.fold_in(key_of[8], 71), 0),
        "outer_velocity": centred(key_of[7], (FRAG,), 0.5, 3.0, ((0, 32),), jnp.float32),
    }


outer_decay = 0.9
outer_stepsize = 0.7


def island_layer(inputs, gate_weight, up_weight, down_weight):
    tokens, cotangent = inputs
    width = FF // N_TP
    gate_value = jnp.dot(tokens, gate_weight, preferred_element_type=jnp.float32)
    up_value = jnp.dot(tokens, up_weight, preferred_element_type=jnp.float32)
    sigmoid_gate = jax.nn.sigmoid(gate_value)
    hidden = (gate_value * sigmoid_gate * up_value).astype(jnp.bfloat16)
    hidden_groups = hidden.astype(jnp.float32).reshape(TOKENS, N_TP, width)
    down_groups = down_weight.astype(jnp.float32).reshape(N_TP, width, D)
    partial_out = jnp.einsum("tgk,gkd->gtd", hidden_groups, down_groups).astype(jnp.bfloat16)
    layer_out = jnp.sum(partial_out.astype(jnp.float32), axis=0).astype(jnp.bfloat16)
    hidden_grad = jnp.dot(cotangent, down_weight.T, preferred_element_type=jnp.float32)
    up_grad = (hidden_grad * gate_value * sigmoid_gate).astype(jnp.bfloat16)
    gate_grad = (hidden_grad * up_value * sigmoid_gate * (1.0 + gate_value * (1.0 - sigmoid_gate))).astype(jnp.bfloat16)
    gate_groups = gate_grad.astype(jnp.float32).reshape(TOKENS, N_TP, width)
    upgrad_groups = up_grad.astype(jnp.float32).reshape(TOKENS, N_TP, width)
    gate_columns = gate_weight.astype(jnp.float32).reshape(D, N_TP, width)
    up_columns = up_weight.astype(jnp.float32).reshape(D, N_TP, width)
    partial_back = jnp.einsum("tgk,dgk->gtd", gate_groups, gate_columns) + jnp.einsum("tgk,dgk->gtd", upgrad_groups, up_columns)
    partial_back = partial_back.astype(jnp.bfloat16)
    input_grad = jnp.sum(partial_back.astype(jnp.float32), axis=0).astype(jnp.bfloat16)
    return layer_out, input_grad


def reference(tokens, cotangent, gate_weight, up_weight, down_weight, local_fragment, global_fragment, outer_velocity):
    layer_out, input_grad = lax.map(
        lambda pair: island_layer(pair, gate_weight, up_weight, down_weight), (tokens, cotangent))
    difference = global_fragment[None, :] - local_fragment
    average = jnp.sum(difference, axis=0) / N_ISLAND
    new_velocity = outer_decay * outer_velocity + average
    new_fragment = global_fragment - outer_stepsize * (average + outer_decay * new_velocity)
    return layer_out, input_grad, new_fragment, new_velocity
```

```python
import jax
import jax.numpy as jnp
from jax import lax
from jax.experimental import pallas as pl
from jax.experimental.pallas import tpu as pltpu
from jax.sharding import PartitionSpec as P

outer_decay = 0.9
outer_stepsize = 0.7

MESH = pl.DeviceIdType.MESH
BF, F32 = jnp.bfloat16, jnp.float32
NX, NYH, NYL, NZ = 4, 4, 2, 12
ISLANDS = NYL * NZ
ROWS, D, WIDTH = 8, 4096, 224
FRAG_ROWS = 192
ZROWS = FRAG_ROWS // NZ
TILE = 512

DYS = (-1, 1, 2, 0)
DXS = (0, -1, 1, 2)


def slot(dy, dx):
    return pl.ds((DYS.index(dy) * 4 + DXS.index(dx)) * ROWS, ROWS)


def nt(a, b):
    return lax.dot_general(a, b, (((1,), (1,)), ((), ())), preferred_element_type=F32)


def nn(a, b):
    return jnp.dot(a, b, preferred_element_type=F32)


def kernel(
    tok, cot, wg, wu, wd, lfrag, gfrag, vel,
    o_layer, o_grad, o_frag, o_vel,
    xc, w, pb, hid, gg, ug, rf, rd, sy, ry, r0, ob,
    fl, fg, fv, rz, s12, sp, av, nf, nv,
    lsem, ssem, rsem, ysem, zsem, zsem2,
):
    island, tp = lax.axis_index("island"), lax.axis_index("tp")
    core, x, yh = lax.rem(tp, 2), lax.rem(tp // 2, NX), tp // (2 * NX)
    yl, z = island // NZ, lax.rem(island, NZ)

    def at(dx=0, dy=0, dz=0, dyl=0, dc=0):
        zz, yy = lax.rem(z + dz + NZ, NZ), lax.rem(yh + dy + NYH, NYH)
        xx = lax.rem(x + dx + NX, NX)
        return (lax.rem(yl + dyl, NYL) * NZ + zz, (yy * NX + xx) * 2 + lax.rem(core + dc, 2))

    copies = {}

    def send(name, src, dst, to):
        k = len(copies)
        copies[name] = pltpu.make_async_remote_copy(
            src_ref=src, dst_ref=dst, send_sem=ssem.at[k], recv_sem=rsem.at[k],
            device_id=to, device_id_type=MESH,
        )
        copies[name].start()

    def recv(*name):
        copies[name].wait_recv()

    def signal(sem, to):
        pl.semaphore_signal(sem, inc=1, device_id=to, device_id_type=MESH)

    loads = []

    def load(src, dst):
        cp = pltpu.make_async_copy(src, dst, lsem.at[len(loads)])
        cp.start()
        loads.append(cp)
        return cp

    barrier = pltpu.get_barrier_semaphore()
    near = [dict(dx=1), dict(dx=-1), dict(dy=1), dict(dy=-1), dict(dc=1), dict(dyl=1)]
    near += [dict(dz=1), dict(dz=-1), dict(dz=2), dict(dz=-2)]
    for k in near:
        signal(barrier, at(**k))
    own = [load(tok.at[0], xc.at[0, slot(0, 0)]), load(cot.at[0], xc.at[1, slot(0, 0)])]
    frag_loads = [load(lfrag, fl), load(gfrag, fg), load(vel, fv)]
    weights = [load(wt, w.at[i, pl.ds(0, WIDTH)]) for i, wt in enumerate((wg, wu, wd))]
    pl.semaphore_wait(barrier, len(near))

    for i, src in ((0, tok), (1, cot)):
        for s in (1, -1):
            send(("x", 0, s, i), src.at[0], xc.at[i, slot(0, -s)], at(dx=s))
        for s in (1, -1):
            send(("y", s, i), src.at[0], xc.at[i, slot(-s, 0)], at(dy=s))
    for s in (1, -1):
        signal(ysem, at(dy=s))
        signal(zsem, at(dz=2 * s))
    for i, wt in enumerate((wg, wu, wd)):
        send(("w", i), wt, w.at[i, pl.ds(WIDTH, WIDTH)], at(dc=1))
    pl.semaphore_wait(ysem, 2)
    for i, src in ((0, tok), (1, cot)):
        send(("y", 2, i), src.at[0], xc.at[i, slot(2, 0)], at(dy=2))
    pl.semaphore_wait(zsem, 2)
    for s in (1, -1):
        signal(zsem2, at(dz=2 * s))

    def spread(dy, i):
        recv("y", 2 if dy == 2 else -dy, i)
        for s in (1, -1):
            send(("x", dy, s, i), xc.at[i, slot(dy, 0)], xc.at[i, slot(dy, -s)], at(dx=s))

    def relay(dy):
        recv("x", dy, 1, 0)
        send(("f", dy, 0), xc.at[0, slot(dy, -1)], xc.at[0, slot(dy, 2)], at(dx=1))
        recv("x", dy, -1, 1)
        send(("f", dy, 1), xc.at[1, slot(dy, 1)], xc.at[1, slot(dy, 2)], at(dx=-1))

    def arrived(dy):
        recv("x", dy, -1, 0)
        recv("x", dy, 1, 1)
        recv("f", dy, 0)
        recv("f", dy, 1)

    for cp in frag_loads:
        cp.wait()
    fl[...] = fg[...] - fl[...]
    pl.semaphore_wait(zsem2, 2)
    for k in range(1, NZ):
        there = lax.rem(z + k, NZ)
        part = pl.ds(pl.multiple_of(there * ZROWS, ZROWS), ZROWS)
        send(("z", k), fl.at[part], rz.at[k - 1], at(dz=k))
    mine = pl.ds(pl.multiple_of(z * ZROWS, ZROWS), ZROWS)

    def outer_sum():
        total = fl[mine, :]
        for k in range(1, NZ):
            recv("z", k)
            total = total + rz[k - 1]
        s12[...] = total
        send(("p",), s12, sp, at(dyl=1))

    def outer_spread():
        recv("p")
        av[mine, :] = (s12[...] + sp[...]) / ISLANDS
        for k in range(1, NZ):
            send(("a", k), av.at[mine], av.at[mine], at(dz=k))

    def outer_update():
        for k in range(1, NZ):
            recv("a", k)
        average = av[...]
        velocity = outer_decay * fv[...] + average
        nv[...] = velocity
        nf[...] = fg[...] - outer_stepsize * (average + outer_decay * velocity)
        return [load(nf, o_frag), load(nv, o_vel)]

    for cp in own:
        cp.wait()
    relay(0)
    for i in (0, 1):
        for dy in (-1, 1):
            spread(dy, i)
    for dy in (-1, 1):
        relay(dy)
    spread(2, 0)
    for cp in weights:
        cp.wait()
    for i in range(3):
        recv("w", i)
    for dy in (-1, 1):
        arrived(dy)

    def gradients(rows, between):
        tokens, cotangent = xc[0, rows, :], xc[1, rows, :]
        gate = nt(tokens, w[0])
        between[0]()
        up = nt(tokens, w[1])
        between[1]()
        grad = nt(cotangent, w[2])
        s = jax.nn.sigmoid(gate)
        hid[...] = (gate * s * up).astype(BF)
        ug[...] = (grad * gate * s).astype(BF)
        gg[...] = (grad * up * s * (1.0 + gate * (1.0 - s))).astype(BF)
        between[2]()

    def tiles(fill):
        @pl.loop(0, D // TILE)
        def _(t):
            fill(pl.ds(pl.multiple_of(t * TILE, TILE), TILE))

    def layer_part(rows):
        def fill(cols):
            pb[0, rows, cols] = nn(hid[...], w[2, :, cols]).astype(BF)

        tiles(fill)

    def grad_part(rows):
        def fill(cols):
            both = nn(gg[...], w[0, :, cols]) + nn(ug[...], w[1, :, cols])
            pb[1, rows, cols] = both.astype(BF)

        tiles(fill)

    def scatter(dys, i):
        ahead = 1 if i == 0 else -1
        for dy in dys:
            k = DYS.index(dy)
            send(("rf", dy, i), pb.at[i, slot(dy, 2)], rf.at[i, k], at(dx=ahead))
            send(("rd", dy, -ahead, i), pb.at[i, slot(dy, -ahead)], rd.at[0, i, k], at(dx=-ahead))

    def add_on(dy, i):
        ahead = 1 if i == 0 else -1
        k = DYS.index(dy)
        recv("rf", dy, i)
        here = slot(dy, ahead)
        pb[i, here, :] = (pb[i, here, :].astype(F32) + rf[i, k].astype(F32)).astype(BF)
        send(("rd", dy, ahead, i), pb.at[i, here], rd.at[1, i, k], at(dx=ahead))

    def line_sum(dy, i):
        k = DYS.index(dy)
        recv("rd", dy, 1, i)
        recv("rd", dy, -1, i)
        total = pb[i, slot(dy, 0), :].astype(F32) + rd[0, i, k].astype(F32)
        total = total + rd[1, i, k].astype(F32)
        if dy == 0:
            r0[i] = total
        else:
            sy[k, i] = total.astype(BF)
            send(("ry", dy, i), sy.at[k, i], ry.at[k, i], at(dy=dy))

    first, second = pl.ds(0, 64), pl.ds(64, 64)

    def nothing():
        pass

    def step_c2():
        spread(2, 1)

    gradients(first, (step_c2, lambda: relay(2), outer_sum))
    layer_part(first)
    scatter((-1, 1), 0)
    grad_part(first)
    scatter((-1, 1), 1)
    outer_spread()
    arrived(0)
    arrived(2)

    def adds():
        for dy in (-1, 1):
            add_on(dy, 0)
            add_on(dy, 1)

    def lines():
        for dy in (-1, 1):
            for i in (0, 1):
                line_sum(dy, i)

    gradients(second, (nothing, adds, nothing))
    layer_part(second)
    scatter((2, 0), 0)
    grad_part(second)
    scatter((2, 0), 1)
    lines()
    stores = outer_update()
    for dy in (2, 0):
        add_on(dy, 0)
        add_on(dy, 1)
    for dy in (2, 0):
        for i in (0, 1):
            line_sum(dy, i)
    for i, out in ((0, o_layer), (1, o_grad)):
        total = r0[i]
        for dy in (-1, 1, 2):
            recv("ry", dy, i)
            total = total + ry[DYS.index(dy), i].astype(F32)
        ob[i] = total.astype(BF)
        stores.append(load(ob.at[i], out.at[0]))
    for cp in copies.values():
        cp.wait_send()
    for cp in stores:
        cp.wait()


def step(tokens, cotangent, gate_weight, up_weight, down_weight, local_fragment, global_fragment, outer_velocity):
    frag = jax.ShapeDtypeStruct((FRAG_ROWS, 128), F32)
    rows = jax.ShapeDtypeStruct((1, ROWS, D), BF)
    sends = 120
    vm = pltpu.VMEM
    layer_out, input_grad, new_fragment, new_velocity = pl.pallas_call(
        kernel,
        out_shape=(rows, rows, frag, frag),
        in_specs=[pl.BlockSpec(memory_space=pl.ANY)] * 8,
        out_specs=[pl.BlockSpec(memory_space=pl.ANY)] * 4,
        scratch_shapes=[
            vm((2, 128, D), BF),
            vm((3, 2 * WIDTH, D), BF),
            vm((2, 128, D), BF),
            vm((64, 2 * WIDTH), BF),
            vm((64, 2 * WIDTH), BF),
            vm((64, 2 * WIDTH), BF),
            vm((2, 4, ROWS, D), BF),
            vm((2, 2, 4, ROWS, D), BF),
            vm((3, 2, ROWS, D), BF),
            vm((3, 2, ROWS, D), BF),
            vm((2, ROWS, D), F32),
            vm((2, ROWS, D), BF),
            vm((FRAG_ROWS, 128), F32),
            vm((FRAG_ROWS, 128), F32),
            vm((FRAG_ROWS, 128), F32),
            vm((NZ - 1, ZROWS, 128), F32),
            vm((ZROWS, 128), F32),
            vm((ZROWS, 128), F32),
            vm((FRAG_ROWS, 128), F32),
            vm((FRAG_ROWS, 128), F32),
            vm((FRAG_ROWS, 128), F32),
            pltpu.SemaphoreType.DMA((16,)),
            pltpu.SemaphoreType.DMA((sends,)),
            pltpu.SemaphoreType.DMA((sends,)),
            pltpu.SemaphoreType.REGULAR,
            pltpu.SemaphoreType.REGULAR,
            pltpu.SemaphoreType.REGULAR,
        ],
        compiler_params=pltpu.CompilerParams(
            collective_id=0, has_side_effects=True, vmem_limit_bytes=67043328
        ),
        name="diloco_step",
    )(
        tokens,
        cotangent,
        gate_weight.T,
        up_weight.T,
        down_weight,
        local_fragment.reshape(FRAG_ROWS, 128),
        global_fragment.reshape(FRAG_ROWS, 128),
        outer_velocity.reshape(FRAG_ROWS, 128),
    )
    return layer_out, input_grad, new_fragment.reshape(-1), new_velocity.reshape(-1)


def solution(mesh):
    in_specs = (
        P("island", "tp", None),
        P("island", "tp", None),
        P(None, "tp"),
        P(None, "tp"),
        P("tp", None),
        P("island", "tp"),
        P("tp"),
        P("tp"),
    )
    out_specs = (P("island", "tp", None), P("island", "tp", None), P("tp"), P("tp"))
    return jax.shard_map(step, mesh=mesh, in_specs=in_specs, out_specs=out_specs, check_vma=False)
```
